32 devices in a mesh: req: 8 (over z, y), kvh: 2 (over x), ffn: 2 (over core).
Axes of the slice: x: 2, y: 2, z: 4, core: 2. Of those that a mesh axis runs over, the one named last changes fastest.
Arguments:
- queries: bfloat16 [8, 64, 8192], P('req', None, 'kvh'), may hold values from -8 to 8
- tree_keys: bfloat16 [8, 64, 1024], P('req', None, 'kvh'), may hold values from -4.5 to 4.5
- tree_token_values: bfloat16 [8, 64, 1024], P('req', None, 'kvh'), may hold values from -6 to 6
- cache_keys: bfloat16 [8, 8, 8192, 128], P('req', 'kvh', 'ffn'), may hold values from -4.5 to 4.5
- cached_value_rows: bfloat16 [8, 8, 8192, 128], P('req', 'kvh', 'ffn'), may hold values from -6 to 6
- lengths: int32 [8], replicated, may hold values from 1 to 8192, 16384 in all
- parents: int32 [8, 64], P('req'), may hold values from 0 to 63, as said below
- residual: float32 [512, 8192], P(('req', 'ffn'), 'kvh'), may hold values from -6 to 6
- out_weight: bfloat16 [8192, 8192], P('kvh', ('req', 'ffn')), may hold values from -0.0625 to 0.0625
- norm_gain: float32 [8192], P('kvh'), may hold values from 0.25 to 1.75
- gate_weight: bfloat16 [8192, 28672], P('kvh', ('req', 'ffn')), may hold values from -0.0625 to 0.0625
- up_weight: bfloat16 [8192, 28672], P('kvh', ('req', 'ffn')), may hold values from -0.0625 to 0.0625
- down_weight: bfloat16 [28672, 8192], P(('req', 'ffn'), 'kvh'), may hold values from -0.03125 to 0.03125
Outputs:
- layer_output: float32 [512, 8192], P(('req', 'ffn'), 'kvh')
The draws below stay inside these ranges and needn't reach their ends.
Inputs may be any that keep to these rules, and one draw needn't show every extreme that they name: parents[r, 0] = 0, and parents[r, i] < i for every node i > 0. The lengths of all requests sum to 16384, and the largest is exactly 8192.
All inputs are finite; a program needn't handle non-finite values.
Results may differ from the reference program's by a relative error of at most 0.003.
Values may be sent and summed in bfloat16 or wider, within the bound.
A program may use at most 128 MiB of HBM per device.

```python
import math
import jax
import jax.numpy as jnp
import numpy as np
from jax import lax

D = 8192
FF = 28672
QUERY_HEADS = 64
KEY_VALUE_HEADS = 8
HEAD_DIMENSION = 128
TREE_NODES = 64
CACHE_SLOTS = 8192
REQUEST_COUNT = 8
TOKENS = 512


def sign_layout(key):
    random_bits = jax.random.randint(jax.random.fold_in(key, 7771), (KEY_VALUE_HEADS, HEAD_DIMENSION), 0, 2)
    return (random_bits * 2 - 1).astype(jnp.float32)


def draw_queries(key, part):
    own_key = jax.random.fold_in(key, 101)
    complete_shape = (REQUEST_COUNT, TREE_NODES, QUERY_HEADS * HEAD_DIMENSION)
    background = jnp.clip(2.0 * jax.random.normal(own_key, complete_shape, jnp.float32), -8.0, 8.0)
    value_pattern = sign_layout(key)
    spread_layout = jnp.repeat(value_pattern, QUERY_HEADS // KEY_VALUE_HEADS, axis=0).reshape(QUERY_HEADS * HEAD_DIMENSION)
    node_ids = jnp.arange(TREE_NODES)
    period = TREE_NODES // 4
    aligned = node_ids % period == TREE_NODES // 8
    strength = 5.6 + (node_ids // period % 3).astype(jnp.float32)
    inserted_entries = strength[:, None] * spread_layout[None, :]
    return jnp.where(aligned[None, :, None], inserted_entries[None], background).astype(jnp.bfloat16)


def draw_cache_keys(key, part):
    own_key = jax.random.fold_in(key, 202)
    complete_shape = (REQUEST_COUNT, KEY_VALUE_HEADS, CACHE_SLOTS, HEAD_DIMENSION)
    background = jnp.clip(jax.random.normal(own_key, complete_shape, jnp.float32), -4.5, 4.5)
    inserted_entries = 4.36 * sign_layout(key)[None, :, None, :]
    first_slot = (jnp.arange(CACHE_SLOTS) == 0)[None, None, :, None]
    return jnp.where(first_slot, inserted_entries, background).astype(jnp.bfloat16)


def draw_tree_keys(key, part):
    own_key = jax.random.fold_in(key, 303)
    complete_shape = (REQUEST_COUNT, TREE_NODES, KEY_VALUE_HEADS * HEAD_DIMENSION)
    background = jnp.clip(jax.random.normal(own_key, complete_shape, jnp.float32), -4.5, 4.5)
    inserted_entries = 4.4 * sign_layout(key).reshape(KEY_VALUE_HEADS * HEAD_DIMENSION)
    root_node = (jnp.arange(TREE_NODES) == 0)[None, :, None]
    return jnp.where(root_node, inserted_entries[None, None, :], background).astype(jnp.bfloat16)


def draw_parents(key, part):
    own_key = jax.random.fold_in(key, 404)
    draws = jax.random.randint(own_key, (REQUEST_COUNT, TREE_NODES), 0, 1 << 20)
    node_ids = jnp.arange(TREE_NODES, dtype=jnp.int32)
    chosen = draws % jnp.maximum(node_ids, 1)[None, :]
    return jnp.where(node_ids[None, :] == 0, 0, chosen).astype(jnp.int32)


def level_of(rng, extent, pieces, low, largest):
    factor_of, own = 1.0, jax.random.fold_in(rng, 6)
    for axis_at, parts in pieces:
        heights = jnp.exp(jax.random.uniform(jax.random.fold_in(own, axis_at), (parts,), jnp.float32, low / len(pieces), largest / len(pieces)))
        factor_of = factor_of * jnp.repeat(heights, extent[axis_at] // parts).reshape([-1 if axis == axis_at else 1 for axis in range(len(extent))])
    return factor_of


def profile(amount, total, reach, slope):
    portions = [(1 << 20) // math.isqrt(standing ** slope) + 1 for standing in range(2, amount + 1)]
    rest, given = total - reach - (amount - 1), [1] * (amount - 1)
    while rest > 0:
        candidates = [i for i in range(amount - 1) if given[i] < reach]
        mass, remaining = sum([portions[i] for i in candidates]), rest
        for i in candidates:
            more = min(reach - given[i], max(1, remaining * portions[i] // mass), rest)
            given[i] = given[i] + more
            rest = rest - more
    return np.array([reach] + given)


def uneven_parts(key, number_of, total, reach, skew):
    if number_of == 2:
        one = jax.random.randint(key, (), max(1, total - reach), min(reach, total - 1) + 1)
        return jnp.stack([one, total - one])
    tallies = jnp.asarray(profile(number_of, total, reach, skew), jnp.int32)
    couples = (number_of - 1) // 2
    giver, taker = tallies[1:1 + 2 * couples:2], tallies[2:2 + 2 * couples:2]
    slack = jnp.minimum(giver - 1, reach - taker)
    moved = jax.random.randint(jax.random.fold_in(key, 1), (couples,), 0, 1 << 20) % (slack + 1)
    tallies = tallies.at[1:1 + 2 * couples:2].set(giver - moved).at[2:2 + 2 * couples:2].set(taker + moved)
    return tallies[jax.random.permutation(jax.random.fold_in(key, 2), number_of)]


def noise(rng, extent, scale, most, shards=(), held_as=jnp.bfloat16):
    factor_of = level_of(rng, extent, shards, -0.22, 0.18) if shards else 1.0
    result = jax.random.normal(rng, extent, jnp.float32) * scale * factor_of
    return jnp.minimum(jnp.maximum(result, -most), most).astype(held_as)


def setup_inputs(seed: int = 0) -> dict:
    seeds = jax.random.split(jax.random.key(seed), 14)
    queries = draw_queries(jax.random.fold_in(seeds[13], 71), 0)
    tree_keys = draw_tree_keys(jax.random.fold_in(seeds[13], 71), 0)
    tree_token_values = noise(seeds[2], (REQUEST_COUNT, TREE_NODES, KEY_VALUE_HEADS * HEAD_DIMENSION), 1.0, 6.0, ((0, 8), (2, 2)))
    cache_keys = draw_cache_keys(jax.random.fold_in(seeds[13], 71), 0)
    cached_value_rows = noise(seeds[4], (REQUEST_COUNT, KEY_VALUE_HEADS, CACHE_SLOTS, HEAD_DIMENSION), 1.0, 6.0, ((0, 8), (1, 2), (2, 2)))
    lengths = uneven_parts(seeds[5], REQUEST_COUNT, REQUEST_COUNT * CACHE_SLOTS // 4, CACHE_SLOTS, 2).astype(jnp.int32)
    parents = draw_parents(jax.random.fold_in(seeds[13], 71), 0)
    residual = noise(seeds[7], (TOKENS, D), 1.0, 6.0, ((0, 16), (1, 2)), jnp.float32)
    out_weight = noise(seeds[8], (QUERY_HEADS * HEAD_DIMENSION, D), (QUERY_HEADS * HEAD_DIMENSION) ** -0.5, 0.0625, ((0, 2), (1, 16)))
    norm_gain = jnp.clip(1.0 + 0.15 * jax.random.normal(seeds[9], (D,), jnp.float32), 0.25, 1.75)
    gate_weight = noise(seeds[10], (D, FF), D ** -0.5, 0.0625, ((0, 2), (1, 16)))
    up_weight = noise(seeds[11], (D, FF), D ** -0.5, 0.0625, ((0, 2), (1, 16)))
    down_weight = noise(seeds[12], (FF, D), FF ** -0.5, 0.03125, ((0, 16), (1, 2)))
    return dict(queries=queries, tree_keys=tree_keys, tree_token_values=tree_token_values, cache_keys=cache_keys, cached_value_rows=cached_value_rows, lengths=lengths, parents=parents, residual=residual, out_weight=out_weight, norm_gain=norm_gain, gate_weight=gate_weight, up_weight=up_weight, down_weight=down_weight)


MASKED = -1e+30
EPSILON = 1e-05

def ancestors(parent_row, node_total):
    node_ids = jnp.arange(node_total, dtype=jnp.int32)
    upward = (parent_row[:, None] == node_ids[None, :]).astype(jnp.float32)
    reachable = jnp.minimum(jnp.eye(node_total, dtype=jnp.float32) + upward, 1.0)
    for repeat_count in range((node_total - 1).bit_length()):
        reachable = jnp.minimum(jnp.dot(reachable, reachable, precision=lax.Precision.HIGHEST), 1.0)
    return reachable > 0.5

def attend_request(inputs):
    query_tile_rows, tree_key_rows, tree_value_block, keys_all, values_all, length, parent_row = inputs
    query_group_width = QUERY_HEADS // KEY_VALUE_HEADS
    score_scale = HEAD_DIMENSION ** (-0.5)
    query_complete = query_tile_rows.astype(jnp.float32).reshape(TREE_NODES, KEY_VALUE_HEADS, query_group_width, HEAD_DIMENSION)
    cache_scores = jnp.einsum('nhgd,hpd->hgnp', query_complete, keys_all.astype(jnp.float32)) * score_scale
    tree_complete = tree_key_rows.astype(jnp.float32).reshape(TREE_NODES, KEY_VALUE_HEADS, HEAD_DIMENSION)
    tree_score_matrix = jnp.einsum('czpk,izk->zpci', query_complete, tree_complete) * score_scale
    positions = jnp.arange(CACHE_SLOTS, dtype=jnp.int32)
    cache_usable = jnp.broadcast_to((positions < length)[None, None, None, :], cache_scores.shape)
    tree_usable = jnp.broadcast_to(ancestors(parent_row, TREE_NODES)[None, None], tree_score_matrix.shape)
    scores = jnp.concatenate([cache_scores, tree_score_matrix], axis=-1)
    usable = jnp.concatenate([cache_usable, tree_usable], axis=-1)
    scores = jnp.where(usable, scores, MASKED)
    highest = lax.optimization_barrier(jnp.max(scores, axis=-1, keepdims=True))
    weights = jnp.where(usable, jnp.exp(scores - highest), 0.0)
    total = lax.optimization_barrier(jnp.sum(weights, axis=-1))
    tree_value_rows = tree_value_block.astype(jnp.float32).reshape(TREE_NODES, KEY_VALUE_HEADS, HEAD_DIMENSION).transpose(1, 0, 2)
    values = jnp.concatenate([values_all.astype(jnp.float32), tree_value_rows], axis=1)
    mixed = jnp.einsum('hgnk,hkd->hgnd', weights, values, precision=lax.Precision.HIGHEST) / total[..., None]
    return mixed.transpose(2, 0, 1, 3).reshape(TREE_NODES, QUERY_HEADS * HEAD_DIMENSION).astype(jnp.bfloat16)

def reference(queries, tree_keys, tree_token_values, cache_keys, cached_value_rows, lengths, parents, residual, out_weight, norm_gain, gate_weight, up_weight, down_weight):
    attention = lax.map(attend_request, (queries, tree_keys, tree_token_values, cache_keys, cached_value_rows, lengths, parents))
    attention = attention.reshape(TOKENS, QUERY_HEADS * HEAD_DIMENSION)
    state = residual + jnp.dot(attention, out_weight, preferred_element_type=jnp.float32)
    mean_square = lax.optimization_barrier(jnp.mean(state * state, axis=1, keepdims=True))
    normed = (state * lax.rsqrt(mean_square + EPSILON) * norm_gain).astype(jnp.bfloat16)
    gate = jnp.dot(normed, gate_weight, preferred_element_type=jnp.float32)
    upward = jnp.dot(normed, up_weight, preferred_element_type=jnp.float32)
    activation = (jax.nn.silu(gate) * upward).astype(jnp.bfloat16)
    return state + jnp.dot(activation, down_weight, preferred_element_type=jnp.float32)
```

```python
import functools
import math

import jax
import jax.numpy as jnp
from jax import lax
from jax.experimental import pallas as pl
from jax.experimental.pallas import tpu as pltpu
from jax.sharding import PartitionSpec as P

MASKED = -1e30
EPSILON = 1e-05


def attend(len_ref, q_ref, tk_ref, tv_ref, k_ref, v_ref, par_ref, o_ref, ml_ref, acc, stat, *, chunk, factor):
    live = len_ref[0]
    tree_live = len_ref[1]
    nodes = q_ref.shape[0]
    size = k_ref.shape[-1]
    group = q_ref.shape[1] // size
    rows = nodes * group
    q = jnp.concatenate([q_ref[:, g * size : (g + 1) * size] for g in range(group)], axis=0)
    acc[...] = jnp.zeros_like(acc)
    stat[0:1, :] = jnp.full((1, rows), MASKED, jnp.float32)
    stat[1:2, :] = jnp.zeros((1, rows), jnp.float32)

    def scores_of(keys):
        return lax.dot_general(keys, q, (((1,), (1,)), ((), ())), preferred_element_type=jnp.float32)

    def absorb(scores, usable, values):
        if usable is not None:
            scores = jnp.where(usable, scores, MASKED)
        old = stat[0:1, :]
        top = jnp.maximum(old, jnp.max(scores, axis=0, keepdims=True))
        weights = jnp.exp2(scores * factor - top * factor)
        if usable is not None:
            weights = jnp.where(usable, weights, 0.0)
        shrink = jnp.exp2((old - top) * factor)
        stat[0:1, :] = top
        stat[1:2, :] = stat[1:2, :] * shrink + jnp.sum(weights, axis=0, keepdims=True)
        acc[...] = acc[...] * shrink + lax.dot_general(
            values, weights.astype(jnp.bfloat16), (((0,), (0,)), ((), ())), preferred_element_type=jnp.float32
        )

    full = live // chunk

    def visit(c, carry):
        at = pl.ds(pl.multiple_of(c * chunk, chunk), chunk)
        absorb(scores_of(k_ref[0, at, :]), None, v_ref[0, at, :])
        return carry

    lax.fori_loop(0, full, visit, 0)

    @pl.when(live > full * chunk)
    def _():
        at = pl.ds(pl.multiple_of(full * chunk, chunk), chunk)
        spot = full * chunk + lax.broadcasted_iota(jnp.int32, (chunk, rows), 0)
        absorb(scores_of(k_ref[0, at, :]), spot < live, v_ref[0, at, :])

    @pl.when(tree_live > 0)
    def _():
        up = lax.broadcasted_iota(jnp.int32, (nodes, nodes), 0)
        across = lax.broadcasted_iota(jnp.int32, (nodes, nodes), 1)
        link = jnp.where(up == par_ref[...], 1.0, 0.0) + jnp.where(up == across, 1.0, 0.0)
        reach = jnp.minimum(link, 1.0)
        for _ in range((nodes - 1).bit_length()):
            half = reach.astype(jnp.bfloat16)
            reach = jnp.minimum(jnp.dot(half, half, preferred_element_type=jnp.float32), 1.0)
        row = lax.broadcasted_iota(jnp.int32, (nodes, rows), 0)
        col = lax.broadcasted_iota(jnp.int32, (nodes, rows), 1)
        spread = jnp.where(lax.rem(col, nodes) == row, 1.0, 0.0).astype(jnp.bfloat16)
        mask = jnp.dot(reach.astype(jnp.bfloat16), spread, preferred_element_type=jnp.float32)
        absorb(scores_of(tk_ref[...]), mask > 0.5, tv_ref[...])

    total = stat[1:2, :]
    out = (acc[...] / jnp.where(total > 0.0, total, 1.0)).T.astype(jnp.bfloat16)
    for g in range(group):
        o_ref[:, g * size : (g + 1) * size] = out[g * nodes : (g + 1) * nodes, :]
    ml_ref[0] = jnp.concatenate([stat[0:1, :] * (size**-0.5), total], axis=0)


def attention_part(queries, tree_keys, tree_values, keys, values, lengths2, parents):
    heads, span, size = keys.shape
    nodes, width = queries.shape
    wide = width // heads
    rows = wide // size * nodes
    chunk = math.gcd(span, 1024)
    body = functools.partial(attend, chunk=chunk, factor=size**-0.5 * math.log2(math.e))
    return pl.pallas_call(
        body,
        out_shape=(
            jax.ShapeDtypeStruct((nodes, width), jnp.bfloat16),
            jax.ShapeDtypeStruct((heads, 2, rows), jnp.float32),
        ),
        grid_spec=pltpu.PrefetchScalarGridSpec(
            num_scalar_prefetch=1,
            grid=(heads,),
            in_specs=[
                pl.BlockSpec((nodes, wide), lambda h, n: (0, h)),
                pl.BlockSpec((nodes, size), lambda h, n: (0, h)),
                pl.BlockSpec((nodes, size), lambda h, n: (0, h)),
                pl.BlockSpec((1, span, size), lambda h, n: (h, 0, 0)),
                pl.BlockSpec((1, span, size), lambda h, n: (h, 0, 0)),
                pl.BlockSpec((1, nodes), lambda h, n: (0, 0)),
            ],
            out_specs=(
                pl.BlockSpec((nodes, wide), lambda h, n: (0, h)),
                pl.BlockSpec((1, 2, rows), lambda h, n: (h, 0, 0)),
            ),
            scratch_shapes=[
                pltpu.VMEM((size, rows), jnp.float32),
                pltpu.VMEM((8, rows), jnp.float32),
            ],
        ),
        compiler_params=pltpu.CompilerParams(dimension_semantics=("arbitrary",)),
    )(lengths2, queries, tree_keys, tree_values, keys, values, parents)


MESH = pl.DeviceIdType.MESH
VMEM_LIMIT = 60 * 1024 * 1024


def split_count(n):
    lo = math.isqrt(n)
    while n % lo:
        lo -= 1
    return n // lo, lo


def ring_peers(n, me):
    return [lax.rem(me + d, n) for d in range(1, n)]


def staged_places(hi_n, lo_n, core_n):
    req = lax.axis_index("req")
    hi, lo, core = req // lo_n, lax.rem(req, lo_n), lax.axis_index("ffn")
    hi_peers = [(h, {"req": h * lo_n + lo}) for h in ring_peers(hi_n, hi)]
    lo_peers = [(b, {"req": hi * lo_n + b}) for b in ring_peers(lo_n, lo)]
    core_peers = [(c, {"ffn": c}) for c in ring_peers(core_n, core)]
    return hi, lo, core, hi_peers, lo_peers, core_peers


def meet(peers):
    barrier = pltpu.get_barrier_semaphore()
    for _, where in peers:
        pl.semaphore_signal(barrier, inc=1, device_id=where, device_id_type=MESH)
    pl.semaphore_wait(barrier, len(peers))


def remote(src, dst, send, recv, where):
    return pltpu.make_async_remote_copy(
        src_ref=src, dst_ref=dst, send_sem=send, recv_sem=recv, device_id=where, device_id_type=MESH
    )


def gather_body(x_ref, out_ref, send, recv, own_sem, *, dims, pieces):
    hi_n, lo_n, core_n = dims
    hi, lo, core, hi_peers, lo_peers, core_peers = staged_places(*dims)
    wide = x_ref.shape[1] // pieces
    meet(hi_peers + lo_peers + core_peers)
    own = pltpu.make_async_copy(x_ref, out_ref.at[hi, lo, core], own_sem)
    own.start()
    first, second, third = [], [], []
    for p in range(pieces):
        cols = pl.ds(p * wide, wide)
        group = []
        for d, (_, where) in enumerate(hi_peers):
            copy = remote(
                x_ref.at[:, cols], out_ref.at[hi, lo, core, :, cols], send.at[p, d], recv.at[p, d], where
            )
            copy.start()
            group.append(copy)
        first.append(group)
    own.wait()
    base = len(hi_peers)
    for step in range(pieces + 1):
        if step < pieces:
            cols = pl.ds(step * wide, wide)
            for copy in first[step]:
                copy.wait_recv()
            group = []
            for d, (_, where) in enumerate(lo_peers):
                part = out_ref.at[:, lo, core, :, cols]
                copy = remote(part, part, send.at[step, base + d], recv.at[step, base + d], where)
                copy.start()
                group.append(copy)
            second.append(group)
        if step > 0:
            p = step - 1
            cols = pl.ds(p * wide, wide)
            for copy in second[p]:
                copy.wait_recv()
            group = []
            for d, (_, where) in enumerate(core_peers):
                at = base + len(lo_peers) + d
                part = out_ref.at[:, :, core, :, cols]
                copy = remote(part, part, send.at[p, at], recv.at[p, at], where)
                copy.start()
                group.append(copy)
            third.append(group)
    for group in third:
        for copy in group:
            copy.wait_recv()
    for group in first + second + third:
        for copy in group:
            copy.wait_send()


def gather_tokens(x, collective_id):
    dims = (*split_count(lax.axis_size("req")), lax.axis_size("ffn"))
    rows, width = x.shape
    pieces = math.gcd(width // 128, 4)
    links = sum(dims) - 3
    vmem = pl.BlockSpec(memory_space=pltpu.VMEM)
    out = pl.pallas_call(
        functools.partial(gather_body, dims=dims, pieces=pieces),
        out_shape=jax.ShapeDtypeStruct((*dims, rows, width), x.dtype),
        in_specs=[vmem],
        out_specs=vmem,
        scratch_shapes=[
            pltpu.SemaphoreType.DMA((pieces, links)),
            pltpu.SemaphoreType.DMA((pieces, links)),
            pltpu.SemaphoreType.DMA,
        ],
        compiler_params=pltpu.CompilerParams(
            collective_id=collective_id, has_side_effects=True, vmem_limit_bytes=VMEM_LIMIT
        ),
    )(x)
    return out.reshape(math.prod(dims) * rows, width)


def scatter_body(x_ref, state_ref, out_ref, got_core, mid, own_mid, got_lo, low, own_low, got_hi, send, recv, *, dims, pieces):
    hi, lo, core, hi_peers, lo_peers, core_peers = staged_places(*dims)
    hi_n, lo_n, core_n = dims
    wide = x_ref.shape[-1] // pieces
    meet(hi_peers + lo_peers + core_peers)
    first, second, third = [], [], []
    for p in range(pieces):
        cols = pl.ds(p * wide, wide)
        group = []
        for d, (c, where) in enumerate(core_peers):
            copy = remote(
                x_ref.at[:, :, c, :, cols], got_core.at[d, :, :, :, cols], send.at[p, d], recv.at[p, d], where
            )
            copy.start()
            group.append(copy)
        first.append(group)
    base_lo = len(core_peers)
    base_hi = base_lo + len(lo_peers)
    for step in range(pieces + 2):
        if step < pieces:
            p = step
            cols = pl.ds(p * wide, wide)
            for copy in first[p]:
                copy.wait_recv()

            def add_core(h, carry):
                for b in range(lo_n):
                    total = x_ref[h, b, core, :, cols]
                    for d in range(core_n - 1):
                        total = total + got_core[d, h, b, :, cols]
                    mid[h, b, :, cols] = total.astype(jnp.bfloat16)
                    own_mid[h, b, :, cols] = total
                return carry

            lax.fori_loop(0, hi_n, add_core, 0)
            group = []
            for d, (b, where) in enumerate(lo_peers):
                at = base_lo + d
                copy = remote(mid.at[:, b, :, cols], got_lo.at[d, :, :, cols], send.at[p, at], recv.at[p, at], where)
                copy.start()
                group.append(copy)
            second.append(group)
        if 1 <= step <= pieces:
            p = step - 1
            cols = pl.ds(p * wide, wide)
            for copy in second[p]:
                copy.wait_recv()

            def add_lo(h, carry):
                total = own_mid[h, lo, :, cols]
                for d in range(lo_n - 1):
                    total = total + got_lo[d, h, :, cols].astype(jnp.float32)
                low[h, :, cols] = total.astype(jnp.bfloat16)
                own_low[h, :, cols] = total
                return carry

            lax.fori_loop(0, hi_n, add_lo, 0)
            group = []
            for d, (h, where) in enumerate(hi_peers):
                at = base_hi + d
                copy = remote(low.at[h, :, cols], got_hi.at[d, :, cols], send.at[p, at], recv.at[p, at], where)
                copy.start()
                group.append(copy)
            third.append(group)
        if step >= 2:
            p = step - 2
            cols = pl.ds(p * wide, wide)
            for copy in third[p]:
                copy.wait_recv()
            total = own_low[hi, :, cols]
            for d in range(hi_n - 1):
                total = total + got_hi[d, :, cols].astype(jnp.float32)
            out_ref[:, cols] = state_ref[:, cols] + total
    for group in first + second + third:
        for copy in group:
            copy.wait_send()


def scatter_tokens(x, state, collective_id):
    dims = (*split_count(lax.axis_size("req")), lax.axis_size("ffn"))
    hi_n, lo_n, core_n = dims
    rows, width = state.shape
    pieces = math.gcd(width // 128, 4)
    links = sum(dims) - 3
    vmem = pl.BlockSpec(memory_space=pltpu.VMEM)
    return pl.pallas_call(
        functools.partial(scatter_body, dims=dims, pieces=pieces),
        out_shape=jax.ShapeDtypeStruct(state.shape, jnp.float32),
        in_specs=[vmem, vmem],
        out_specs=vmem,
        scratch_shapes=[
            pltpu.VMEM((core_n - 1, hi_n, lo_n, rows, width), jnp.float32),
            pltpu.VMEM((hi_n, lo_n, rows, width), jnp.bfloat16),
            pltpu.VMEM((hi_n, lo_n, rows, width), jnp.float32),
            pltpu.VMEM((lo_n - 1, hi_n, rows, width), jnp.bfloat16),
            pltpu.VMEM((hi_n, rows, width), jnp.bfloat16),
            pltpu.VMEM((hi_n, rows, width), jnp.float32),
            pltpu.VMEM((hi_n - 1, rows, width), jnp.bfloat16),
            pltpu.SemaphoreType.DMA((pieces, links)),
            pltpu.SemaphoreType.DMA((pieces, links)),
        ],
        compiler_params=pltpu.CompilerParams(
            collective_id=collective_id, has_side_effects=True, vmem_limit_bytes=VMEM_LIMIT
        ),
    )(x.reshape(*dims, rows, width), state)


def gated_body(gate_ref, up_ref, own_gate_ref, own_up_ref, out_ref, got_gate, got_up, send, recv, *, pieces):
    n = gate_ref.shape[0]
    rows = gate_ref.shape[1]
    me = lax.axis_index("kvh")
    peers = [(k, {"kvh": k}) for k in ring_peers(n, me)]
    wide = gate_ref.shape[2] // pieces
    meet(peers)
    first, second = [], []
    for p in range(pieces):
        cols = pl.ds(p * wide, wide)
        group = []
        for d, (k, where) in enumerate(peers):
            for half, (src, dst) in enumerate(((gate_ref, got_gate), (up_ref, got_up))):
                copy = remote(
                    src.at[k, :, cols], dst.at[d, :, cols], send.at[half, p, d], recv.at[half, p, d], where
                )
                copy.start()
                group.append(copy)
        first.append(group)
    for p in range(pieces):
        cols = pl.ds(p * wide, wide)
        for copy in first[p]:
            copy.wait_recv()
        step = math.gcd(rows, 64)

        def activate(r, carry):
            at = pl.ds(pl.multiple_of(r * step, step), step)
            gate = own_gate_ref[at, cols]
            up = own_up_ref[at, cols]
            for d in range(n - 1):
                gate = gate + got_gate[d, at, cols].astype(jnp.float32)
                up = up + got_up[d, at, cols].astype(jnp.float32)
            out_ref[me, at, cols] = (gate / (1.0 + jnp.exp(-gate)) * up).astype(jnp.bfloat16)
            return carry

        lax.fori_loop(0, rows // step, activate, 0)
        group = []
        for d, (_, where) in enumerate(peers):
            part = out_ref.at[me, :, cols]
            copy = remote(part, part, send.at[2, p, d], recv.at[2, p, d], where)
            copy.start()
            group.append(copy)
        second.append(group)
    for group in second:
        for copy in group:
            copy.wait_recv()
    for group in first + second:
        for copy in group:
            copy.wait_send()


def gated(gate, up, collective_id):
    n = lax.axis_size("kvh")
    tokens, width = gate.shape
    rows = tokens // n
    pieces = math.gcd(width // 128, 7)
    gate, up = gate.reshape(n, rows, width), up.reshape(n, rows, width)
    me = lax.axis_index("kvh")
    own_gate = lax.dynamic_index_in_dim(gate, me, keepdims=False)
    own_up = lax.dynamic_index_in_dim(up, me, keepdims=False)
    vmem = pl.BlockSpec(memory_space=pltpu.VMEM)
    out = pl.pallas_call(
        functools.partial(gated_body, pieces=pieces),
        out_shape=jax.ShapeDtypeStruct((n, rows, width), jnp.bfloat16),
        in_specs=[vmem] * 4,
        out_specs=vmem,
        scratch_shapes=[
            pltpu.VMEM((n - 1, rows, width), jnp.bfloat16),
            pltpu.VMEM((n - 1, rows, width), jnp.bfloat16),
            pltpu.SemaphoreType.DMA((3, pieces, n - 1)),
            pltpu.SemaphoreType.DMA((3, pieces, n - 1)),
        ],
        compiler_params=pltpu.CompilerParams(
            collective_id=collective_id, has_side_effects=True, vmem_limit_bytes=VMEM_LIMIT
        ),
    )(gate.astype(jnp.bfloat16), up.astype(jnp.bfloat16), own_gate, own_up)
    return out.reshape(tokens, width)


def local(
    queries,
    tree_keys,
    tree_token_values,
    cache_keys,
    cached_value_rows,
    lengths,
    parents,
    residual,
    out_weight,
    norm_gain,
    gate_weight,
    up_weight,
    down_weight,
):
    heads, half_len, size = cache_keys.shape[1:]
    nodes = queries.shape[1]
    group = queries.shape[2] // (heads * size)
    request_index = lax.axis_index("req")
    half_index = lax.axis_index("ffn")
    halves = lax.axis_size("ffn")
    features = norm_gain.shape[0] * lax.axis_size("kvh")
    length = lax.dynamic_index_in_dim(lengths, request_index, keepdims=False)
    live_len = jnp.clip(length - half_index * half_len, 0, half_len)
    lengths2 = jnp.stack([live_len, (half_index == 0).astype(jnp.int32)])
    own, ml = attention_part(
        queries[0], tree_keys[0], tree_token_values[0], cache_keys[0], cached_value_rows[0], lengths2, parents
    )
    mine_rows = nodes // halves
    pair = lax.all_to_all(own, "ffn", split_axis=0, concat_axis=0, tiled=True).reshape(halves, mine_rows, -1)
    ml_pair = lax.all_gather(ml, "ffn")
    weights = ml_pair[:, :, 1] * jnp.exp(ml_pair[:, :, 0] - jnp.max(ml_pair[:, :, 0], axis=0))
    share = (weights / jnp.sum(weights, axis=0)).reshape(halves, heads * group, nodes)
    share = lax.dynamic_slice_in_dim(share, half_index * mine_rows, mine_rows, 2).transpose(0, 2, 1)[..., None]
    mixed = jnp.sum(pair.astype(jnp.float32).reshape(halves, mine_rows, heads * group, size) * share, axis=0)
    attention = mixed.astype(jnp.bfloat16).reshape(mine_rows, heads * group * size)
    partial_rows = jnp.dot(gather_tokens(attention, 1), out_weight, preferred_element_type=jnp.float32)
    regrouped = lax.all_to_all(
        partial_rows, ("req", "ffn"), split_axis=0, concat_axis=1, tiled=True
    )
    shares = lax.all_to_all(regrouped, "kvh", split_axis=1, concat_axis=0, tiled=True)
    projected = jnp.sum(shares.reshape(-1, *residual.shape), axis=0)
    state = residual + projected
    squares = lax.psum(jnp.sum(state * state, axis=1), "kvh")
    normed = (state * lax.rsqrt(squares / features + EPSILON)[:, None] * norm_gain).astype(jnp.bfloat16)
    block_rows = gather_tokens(normed, 2)
    gate_part = jnp.dot(block_rows, gate_weight, preferred_element_type=jnp.float32)
    up_part = jnp.dot(block_rows, up_weight, preferred_element_type=jnp.float32)
    activation = gated(gate_part, up_part, 3)
    down_part = jnp.dot(activation, down_weight, preferred_element_type=jnp.float32)
    return scatter_tokens(down_part, state, 4)


def solution(mesh):
    in_specs = (
        P("req", None, "kvh"),
        P("req", None, "kvh"),
        P("req", None, "kvh"),
        P("req", "kvh", "ffn", None),
        P("req", "kvh", "ffn", None),
        P(),
        P("req", None),
        P(("req", "ffn"), "kvh"),
        P("kvh", ("req", "ffn")),
        P("kvh"),
        P("kvh", ("req", "ffn")),
        P("kvh", ("req", "ffn")),
        P(("req", "ffn"), "kvh"),
    )
    out_specs = P(("req", "ffn"), "kvh")
    return jax.shard_map(local, mesh=mesh, in_specs=in_specs, out_specs=out_specs, check_vma=False)
```
